32 devices in a mesh: grp: 2 (over y), span: 4 (over z), tm: 2 (over x), head: 2 (over core).
Axes of the slice: x: 2, y: 2, z: 4, core: 2. Of those that a mesh axis runs over, the one named last changes fastest.
Arguments:
- frames: bfloat16 [8, 256, 768], P(('grp', 'span'), 'tm'), parts along dimension 0, may hold values from -6 to 6
- levels: int32 [8], P(('grp', 'span')), parts along dimension 0, may hold values from 0 to 15
- owners: int32 [4], P('grp'), parts along dimension 0, may hold values from 0 to 3, as said below
- person_ids: int32 [8, 256], P(('grp', 'span'), 'tm'), parts along dimension 0, may hold values from 0 to 3
- w_qkv: bfloat16 [3, 768, 768], P(None, None, 'head'), may hold values from -1 to 1
- w_out: bfloat16 [768, 768], P('head'), may hold values from -0.21875 to 0.21875
- w_up: bfloat16 [768, 3072], P('tm', 'head'), may hold values from -0.21875 to 0.21875
- w_down: bfloat16 [3072, 768], P('head', 'tm'), may hold values from -0.109375 to 0.109375
- level_table: bfloat16 [16, 768], replicated, may hold values from -3 to 3
- person_table: bfloat16 [4, 768], replicated, may hold values from -3 to 3
- blend_rates: float32 [16], replicated, may hold values from 0.25 to 1
Outputs:
- denoised: bfloat16 [8, 256, 768], P(('grp', 'span'), 'tm'), parts along dimension 0
The draws below stay inside these ranges and needn't reach their ends.
There are 2 independent parts, one for each index of `grp`. The reference program is written for one: setup_inputs(seed, part) draws one part's arguments, and reference() takes and returns one part's arrays. A program takes and returns all parts, laid end to end along the dimension named above; an argument that names none is the same for every part. Nothing has to cross between parts.
Inputs may be any that keep to these rules, and one draw needn't show every extreme that they name: `owners`: the owner of step s + 1 is the span after the owner of step s around the loop.
All inputs are finite; a program needn't handle non-finite values.
Results may differ from the reference program's by a relative error of at most 0.011.
Values may be sent and summed in bfloat16 or wider, within the bound.
A program may use at most 64 MiB of HBM per device.

```python
import math
import jax
import jax.numpy as jnp
from jax import lax

D = 768
HEADS = 12
HD = 64
FF = 3072
PERSONS = 4
LEVELS = 16
STEPS = 2
SPANS = 4
FR = 256


def draw_owners(key, part):
    first_owner = jax.random.randint(key, (), 0, SPANS)
    return ((first_owner + jnp.arange(STEPS, dtype=jnp.int32)) % SPANS).astype(jnp.int32)


def draw_w_qkv(key, part):
    key_base = jax.random.fold_in(key, 0)
    base = jax.random.normal(key_base, (3, D, D), jnp.float32)
    norm_factor = 1.0 / jnp.sqrt(jnp.float32(D))
    stacked = jnp.stack([base[0] * (1.6 * norm_factor), base[1] * (1.6 * norm_factor), base[2] * norm_factor])
    return jnp.clip(stacked, -1.0, 1.0).astype(jnp.bfloat16)


def touch_ends(array, rng, low, largest):
    spot = [jax.random.randint(jax.random.fold_in(rng, axis), (), 0, length) for axis, length in enumerate(array.shape)]
    widest = array.shape.index(max(array.shape))
    neighbour = spot[:widest] + [(spot[widest] + 1) % array.shape[widest]] + spot[widest + 1:]
    return array.at[tuple(spot)].set(low).at[tuple(neighbour)].set(largest)


def block_levels(stream_key, extent, cuts, least, top_value):
    factor_of, own = 1.0, jax.random.fold_in(stream_key, 6)
    for dim, shards_of in cuts:
        draws = jnp.exp(jax.random.uniform(jax.random.fold_in(own, dim), (shards_of,), jnp.float32, least / len(cuts), top_value / len(cuts)))
        factor_of = factor_of * jnp.repeat(draws, extent[dim] // shards_of).reshape([-1 if axis == dim else 1 for axis in range(len(extent))])
    return factor_of


def centred(key, dims, deviation, most, shards=(), kind=jnp.bfloat16):
    values = deviation * jax.random.normal(key, dims, jnp.float32)
    if shards:
        values = values * block_levels(key, dims, shards, -0.22, 0.18)
    return jnp.clip(values, -most, most).astype(kind)


def setup_inputs(seed: int = 0, part: int = 0) -> dict:
    arg_keys = jax.random.split(jax.random.key(seed), 12)
    part_keys = jax.random.split(jax.random.fold_in(arg_keys[11], part), 12)
    frames = centred(part_keys[0], (SPANS, FR, D), 1.0, 6.0, ((0, 4), (1, 2)))
    levels = touch_ends(jax.random.randint(part_keys[1], (SPANS,), 0, LEVELS), jax.random.fold_in(part_keys[1], 1), 0, LEVELS - 1).astype(jnp.int32)
    owners = draw_owners(jax.random.fold_in(jax.random.fold_in(arg_keys[11], part), 71), part)
    person_ids = touch_ends(jax.random.randint(part_keys[3], (SPANS, FR), 0, PERSONS), jax.random.fold_in(part_keys[3], 1), 0, PERSONS - 1).astype(jnp.int32)
    w_qkv = draw_w_qkv(jax.random.fold_in(arg_keys[11], 71), part)
    w_out = centred(arg_keys[5], (D, D), D ** -0.5, 0.21875, ((0, 2),))
    w_up = centred(arg_keys[6], (D, FF), D ** -0.5, 0.21875, ((0, 2), (1, 2)))
    w_down = centred(arg_keys[7], (FF, D), FF ** -0.5, 0.109375, ((0, 2), (1, 2)))
    level_table = centred(arg_keys[8], (LEVELS, D), 0.5, 3.0)
    person_table = centred(arg_keys[9], (PERSONS, D), 0.5, 3.0)
    blend_rates = jnp.clip(jnp.exp(jax.random.uniform(arg_keys[10], (LEVELS,), jnp.float32, math.log(0.25), math.log(1.0))), 0.25, 1.0)
    return {"frames": frames, "levels": levels, "owners": owners, "person_ids": person_ids, "w_qkv": w_qkv, "w_out": w_out, "w_up": w_up, "w_down": w_down, "level_table": level_table, "person_table": person_table, "blend_rates": blend_rates}


EPSILON = 1e-05

def layer_norm(values):
    center = values - lax.optimization_barrier(jnp.mean(values, axis=-1, keepdims=True))
    spread = lax.optimization_barrier(jnp.mean(center * center, axis=-1, keepdims=True))
    return center * lax.rsqrt(spread + EPSILON)

def attend_span(queries, keys, values):
    scores = jnp.einsum('qhd,khd->hqk', queries.astype(jnp.float32), keys.astype(jnp.float32)) * (1.0 / math.sqrt(queries.shape[2]))
    top = lax.optimization_barrier(jnp.max(scores, axis=2, keepdims=True))
    weights = jnp.exp(scores - top)
    totals = lax.optimization_barrier(jnp.sum(weights, axis=2))
    rounded = lax.optimization_barrier(weights.astype(jnp.bfloat16))
    mixed = jnp.einsum('hqk,khd->hqd', rounded.astype(jnp.float32), values.astype(jnp.float32)) / totals[:, :, None]
    return jnp.transpose(mixed, (1, 0, 2)).reshape(queries.shape[0], -1).astype(jnp.bfloat16)

def reference(frames, levels, owners, person_ids, w_qkv, w_out, w_up, w_down, level_table, person_table, blend_rates):
    embed = level_table[levels].astype(jnp.float32)[:, None, :] + person_table[person_ids].astype(jnp.float32)
    blend = blend_rates[levels][:, None, None]
    state = frames
    for step_index in range(STEPS):
        hidden_in = state.astype(jnp.float32) + embed
        normed = layer_norm(hidden_in).astype(jnp.bfloat16).reshape(SPANS * FR, D)
        projected = tuple((jnp.dot(normed, w_qkv[slot_index], preferred_element_type=jnp.float32).astype(jnp.bfloat16) for slot_index in range(3)))
        projected = lax.optimization_barrier(projected)
        queries, keys, values = [piece.reshape(SPANS, FR, HEADS, HD) for piece in projected]
        owner_index = owners[step_index]
        clean_keys = lax.dynamic_index_in_dim(keys, owner_index, 0, keepdims=False)
        clean_values = lax.dynamic_index_in_dim(values, owner_index, 0, keepdims=False)

        def per_span(items):
            span_queries, span_keys, span_values = items
            return attend_span(span_queries, jnp.concatenate([span_keys, clean_keys], axis=0), jnp.concatenate([span_values, clean_values], axis=0))
        mixed = lax.map(per_span, (queries, keys, values))
        after_attn = hidden_in + jnp.dot(mixed.reshape(SPANS * FR, D), w_out, preferred_element_type=jnp.float32).reshape(SPANS, FR, D)
        normed_two = layer_norm(after_attn).astype(jnp.bfloat16).reshape(SPANS * FR, D)
        activated = jax.nn.gelu(jnp.dot(normed_two, w_up, preferred_element_type=jnp.float32), approximate=True).astype(jnp.bfloat16)
        after_mlp = after_attn + jnp.dot(activated, w_down, preferred_element_type=jnp.float32).reshape(SPANS, FR, D)
        previous = state.astype(jnp.float32)
        state = (previous + blend * (after_mlp - previous)).astype(jnp.bfloat16)
        state = lax.optimization_barrier(state)
    return state
```

```python
import functools
import math

import jax
import jax.numpy as jnp
from jax import lax
from jax.experimental import pallas as pl
from jax.experimental.pallas import tpu as pltpu
from jax.sharding import PartitionSpec as P

HD = 64
STEPS = 2
EPSILON = 1e-05
VMEM = pl.BlockSpec(memory_space=pltpu.VMEM)
SMEM = pl.BlockSpec(memory_space=pltpu.SMEM)


def layer_norm(values):
    center = values - jnp.mean(values, axis=-1, keepdims=True)
    spread = jnp.mean(center * center, axis=-1, keepdims=True)
    return center * lax.rsqrt(spread + EPSILON)


def project_rows(blocks, w_ref, out_ref):
    width = w_ref.shape[2]
    start = 0
    for block in blocks:
        rows = slice(start, start + block.shape[0])
        start += block.shape[0]
        for part in (1, 2):
            out_ref[rows, (part - 1) * width : part * width] = jnp.dot(
                block[...], w_ref[part], preferred_element_type=jnp.float32
            ).astype(jnp.bfloat16)


def project_kernel(w_ref, mine_ref, *refs):
    *blocks, q_ref, kv_ref = refs
    q_ref[...] = jnp.dot(
        mine_ref[...], w_ref[0], preferred_element_type=jnp.float32
    ).astype(jnp.bfloat16)
    project_rows(blocks, w_ref, kv_ref)


def project(w_qkv, mine, blocks):
    model, width = w_qkv.shape[1:]
    rows = mine.shape[0]
    keys = sum(block.shape[0] for block in blocks)
    return pl.pallas_call(
        project_kernel,
        out_shape=(
            jax.ShapeDtypeStruct((rows, width), jnp.bfloat16),
            jax.ShapeDtypeStruct((keys, 2 * width), jnp.bfloat16),
        ),
        in_specs=[VMEM] * (2 + len(blocks)),
        out_specs=(VMEM, VMEM),
        cost_estimate=pl.CostEstimate(
            flops=2 * model * width * (rows + 2 * keys),
            bytes_accessed=2 * (3 * model * width + (rows + keys) * (model + 2 * width)),
            transcendentals=0,
        ),
        name="project",
    )(w_qkv, mine, *blocks)


def attend(q_ref, panels, mixed_ref):
    width = q_ref.shape[1]
    for head in range(width // HD):
        keys = slice(head * HD, (head + 1) * HD)
        vals = slice(width + head * HD, width + (head + 1) * HD)
        query = q_ref[:, keys]
        scores = [
            lax.dot_general(
                query, panel[:, keys], (((1,), (1,)), ((), ())), preferred_element_type=jnp.float32
            )
            * (1.0 / math.sqrt(HD))
            for panel in panels
        ]
        top = functools.reduce(
            jnp.maximum, [jnp.max(score, axis=1, keepdims=True) for score in scores]
        )
        total = 0.0
        mixed = 0.0
        for score, panel in zip(scores, panels):
            weights = jnp.exp(score - top)
            total += jnp.sum(weights, axis=1, keepdims=True)
            mixed += jnp.dot(
                weights.astype(jnp.bfloat16), panel[:, vals], preferred_element_type=jnp.float32
            )
        mixed_ref[:, keys] = (mixed / total).astype(jnp.bfloat16)


def feed_forward(normed_ref, up, down, ups, downs, part_ref):
    if not ups:
        value = jnp.dot(normed_ref[...], up[...], preferred_element_type=jnp.float32)
        activated = jax.nn.gelu(value, approximate=True).astype(jnp.bfloat16)
        part_ref[...] = jnp.dot(
            activated, down[...], preferred_element_type=jnp.float32
        ).astype(jnp.bfloat16)
        return
    depth, size = ups[0].shape
    slab, grp = lax.axis_index("tm"), lax.axis_index("grp")
    here = pl.ds(pl.multiple_of(slab * depth, 128), depth)
    there = pl.ds(pl.multiple_of((1 - slab) * depth, 128), depth)
    near, far = normed_ref[:, here], normed_ref[:, there]
    near_sum = 0.0
    far_sum = 0.0
    for i in range(4):
        place = 2 * (grp if i % 2 == 0 else 1 - grp) + i // 2
        units = pl.ds(pl.multiple_of(place * size, 128), size)
        value = jnp.dot(near, up[:, units], preferred_element_type=jnp.float32) + jnp.dot(
            far, ups[i][...], preferred_element_type=jnp.float32
        )
        activated = jax.nn.gelu(value, approximate=True).astype(jnp.bfloat16)
        near_sum += jnp.dot(activated, down[units, :], preferred_element_type=jnp.float32)
        far_sum += jnp.dot(activated, downs[i][...], preferred_element_type=jnp.float32)
    part_ref[:, here] = near_sum.astype(jnp.bfloat16)
    part_ref[:, there] = far_sum.astype(jnp.bfloat16)


def layer_kernel(
    contexts, chunks, last, blend_ref, q_ref, own_ref, w_qkv_ref, w_out_ref, state_ref, hidden_ref, *refs
):
    refs = list(refs)
    embed_ref = None if last else refs.pop(0)
    blocks = [refs.pop(0) for _ in range(contexts)]
    far_weights = [refs.pop(0) for _ in range(2 + 2 * chunks)]
    state_out = refs.pop(0)
    if not last:
        hidden_out, normed_out = refs.pop(0), refs.pop(0)
    context_ref, mixed_ref, normed_ref, sent, got, send_sem, recv_sem, load_sem = refs[:8]
    weights = refs[8:]
    peer = {"head": 1 - lax.axis_index("head")}

    barrier = pltpu.get_barrier_semaphore()
    pl.semaphore_signal(barrier, inc=1, device_id=peer, device_id_type=pl.DeviceIdType.MESH)
    loads = [
        pltpu.make_async_copy(far_weights[i], weights[i], load_sem.at[i])
        for i in range(len(weights))
    ]
    for load in loads:
        load.start()
    pl.semaphore_wait(barrier, 1)

    def exchange(turn):
        return pltpu.make_async_remote_copy(
            src_ref=sent.at[turn],
            dst_ref=got.at[turn],
            send_sem=send_sem.at[turn],
            recv_sem=recv_sem.at[turn],
            device_id=peer,
            device_id_type=pl.DeviceIdType.MESH,
        )

    project_rows(blocks, w_qkv_ref, context_ref)
    attend(q_ref, (own_ref, context_ref), mixed_ref)
    sent[0] = jnp.dot(
        mixed_ref[...], w_out_ref[...], preferred_element_type=jnp.float32
    ).astype(jnp.bfloat16)
    copy = exchange(0)
    copy.start()
    for load in loads:
        load.wait()
    copy.wait()
    after = hidden_ref[...] + (sent[0].astype(jnp.float32) + got[0].astype(jnp.float32))
    normed_ref[...] = layer_norm(after).astype(jnp.bfloat16)
    feed_forward(
        normed_ref,
        weights[0],
        weights[1],
        weights[2 : 2 + chunks],
        weights[2 + chunks :],
        sent.at[1],
    )
    copy = exchange(1)
    copy.start()
    copy.wait()
    after = after + (sent[1].astype(jnp.float32) + got[1].astype(jnp.float32))
    previous = state_ref[...].astype(jnp.float32)
    state = (previous + blend_ref[0] * (after - previous)).astype(jnp.bfloat16)
    state_out[...] = state
    if not last:
        hidden = state.astype(jnp.float32) + embed_ref[...]
        hidden_out[...] = hidden
        normed_out[...] = layer_norm(hidden).astype(jnp.bfloat16)


def layer(blend, queries, own, w_qkv, w_out, state, hidden, embed, blocks, weights):
    rows, width = queries.shape
    model = w_out.shape[1]
    extra = sum(block.shape[0] for block in blocks)
    keys = own.shape[0] + extra
    last = not embed
    inner = w_qkv.shape[2] * 4
    small = jax.ShapeDtypeStruct((rows, model), jnp.bfloat16)
    shapes = (small,) if last else (small, jax.ShapeDtypeStruct((rows, model), jnp.float32), small)
    return pl.pallas_call(
        functools.partial(layer_kernel, len(blocks), (len(weights) - 2) // 2, last),
        out_shape=shapes,
        in_specs=[SMEM]
        + [VMEM] * (6 + len(embed) + len(blocks))
        + [pl.BlockSpec(memory_space=pl.ANY)] * len(weights),
        out_specs=(VMEM,) * len(shapes),
        scratch_shapes=[
            pltpu.VMEM((extra, 2 * width), jnp.bfloat16),
            pltpu.VMEM((rows, width), jnp.bfloat16),
            pltpu.VMEM((rows, model), jnp.bfloat16),
            pltpu.VMEM((2, rows, model), jnp.bfloat16),
            pltpu.VMEM((2, rows, model), jnp.bfloat16),
            pltpu.SemaphoreType.DMA((2,)),
            pltpu.SemaphoreType.DMA((2,)),
            pltpu.SemaphoreType.DMA((len(weights),)),
        ]
        + [pltpu.VMEM(weight.shape, weight.dtype) for weight in weights],
        compiler_params=pltpu.CompilerParams(
            collective_id=1 if last else 0, has_side_effects=True
        ),
        cost_estimate=pl.CostEstimate(
            flops=4 * rows * keys * width
            + (2 * rows + 4 * extra) * width * model
            + 4 * rows * model * inner,
            bytes_accessed=2 * (2 * keys * width + 4 * width * model)
            + 4 * model * inner
            + 20 * rows * model,
            transcendentals=rows * keys * width // HD + rows * inner,
        ),
        name="layer_last" if last else "layer",
    )(blend.reshape(1), queries, own, w_qkv, w_out, state, hidden, *embed, *blocks, *weights)


def swap(block, axis):
    return lax.ppermute(block, axis, [(0, 1), (1, 0)])


def tied(value, *others):
    return lax.optimization_barrier((value, *others))[0] if others else value


def from_owner(mine, owner, spans, ties=()):
    span = lax.axis_index("span")
    if spans & (spans - 1):
        return lax.psum(jnp.where(span == owner, mine, jnp.zeros_like(mine)), "span")
    for bit in range(spans.bit_length() - 1):
        pairs = [(i, i ^ (1 << bit)) for i in range(spans)]
        arrived = lax.ppermute(mine, "span", pairs)
        mine = jnp.where((owner >> bit) == (span >> bit), mine, arrived)
        mine = tied(mine, *ties[bit : bit + 1])
    return mine


def owner_quarters(normed, owner, spans, slabs):
    rows = normed.shape[0] // 2
    mine = lax.dynamic_slice_in_dim(normed, lax.axis_index("head") * rows, rows, 0)
    mine = from_owner(mine, owner, spans)
    if slabs != 2:
        return [lax.all_gather(mine, ("tm", "head"), axis=0, tiled=True)]
    return [mine] + [
        lax.ppermute(mine, ("tm", "head"), [(i, i ^ k) for i in range(4)]) for k in (1, 2, 3)
    ]


def owner_halves(mine, other, owner, spans, ties):
    same = lax.axis_index("tm") == lax.axis_index("head")
    half = from_owner(jnp.where(same, mine, other), owner, spans, ties)
    return [half, swap(half, "head")]


def relayed(weight, axis, place, size):
    got = swap(lax.dynamic_slice_in_dim(weight, place, size, axis), "tm")
    return [got, swap(got, "grp")]


LANES = 128
INFO = 32
NT = (((1,), (1,)), ((), ()))
TN = (((0,), (0,)), ((), ()))
Z, X, CA, CB, W, HX = 0, 3, 7, 10, 14, 30
COPIES = 36
UP_ROWS, DOWN_ROWS = 48, 192


def dot(a, b, dims=None):
    if dims is None:
        return jnp.dot(a, b, preferred_element_type=jnp.float32)
    return lax.dot_general(a, b, dims, preferred_element_type=jnp.float32)


def fused_kernel(
    owners_ref,
    levels_ref,
    rates_ref,
    ids_ref,
    frames_ref,
    level_ref,
    person_ref,
    qkv_hbm,
    out_hbm,
    up_hbm,
    down_hbm,
    result_ref,
    items,
    table,
    qkv_w,
    out_w,
    up_w,
    down_w,
    hidden,
    after_state,
    normed,
    ctx_normed,
    queries,
    kv,
    mixed,
    act,
    sent,
    got,
    send_sem,
    recv_sem,
    load_sem,
):
    bf16, f32 = jnp.bfloat16, jnp.float32
    y, s = lax.axis_index("grp"), lax.axis_index("span")
    t, h = lax.axis_index("tm"), lax.axis_index("head")
    half = frames_ref.shape[1]
    quarter = half // 2
    rows = 2 * half
    model = frames_ref.shape[2]
    width = out_hbm.shape[0]
    depth = up_hbm.shape[0]
    blocks = model // LANES
    low = lax.rem(s, 2)
    spans = {1: s + 1 - 2 * low, 2: lax.rem(s + 2, 4), 3: 3 - s}
    peer_x, peer_y, peer_c = {"tm": 1 - t}, {"grp": 1 - y}, {"head": 1 - h}
    peer_z = {k: {"span": spans[k]} for k in spans}

    barrier = pltpu.get_barrier_semaphore()
    for peer in (peer_c, peer_x, peer_y, *peer_z.values()):
        pl.semaphore_signal(barrier, inc=1, device_id=peer, device_id_type=pl.DeviceIdType.MESH)

    near = pl.ds(pl.multiple_of(t * depth, LANES), depth)
    far = pl.ds(pl.multiple_of((1 - t) * depth, LANES), depth)
    loads = [
        pltpu.make_async_copy(qkv_hbm.at[i], qkv_w.at[:, i * width : (i + 1) * width], load_sem.at[i])
        for i in range(3)
    ] + [
        pltpu.make_async_copy(out_hbm, out_w, load_sem.at[3]),
        pltpu.make_async_copy(up_hbm, up_w.at[near, :], load_sem.at[4]),
        pltpu.make_async_copy(down_hbm, down_w.at[:, near], load_sem.at[5]),
    ]
    for load in loads:
        load.start()

    for part in range(2):
        for c in range(blocks):
            items[s, t, part, c * quarter : (c + 1) * quarter, :] = frames_ref[
                0, part * quarter : (part + 1) * quarter, c * LANES : (c + 1) * LANES
            ]
    place = lax.broadcasted_iota(jnp.int32, (INFO, half), 0)
    hot = jnp.where(place < 16, place, place - 16) == jnp.where(place < 16, levels_ref[0], ids_ref[...])
    info = jnp.where(hot, 1.0, 0.0).astype(bf16)
    for part in range(2):
        items[s, t, part, blocks * quarter :, :] = info
    table[0:16, :] = level_ref[...]
    person = person_ref[...].astype(f32)
    line = lax.broadcasted_iota(jnp.int32, (16, model), 0)
    lower = jnp.zeros((16, model), f32)
    for p in range(person_ref.shape[0]):
        lower = jnp.where(line == p, person[p : p + 1, :], lower)
    table[16:32, :] = lower.astype(bf16)
    line = lax.broadcasted_iota(jnp.int32, (16, LANES), 0)
    rates = jnp.zeros((16, LANES), f32)
    for p in range(16):
        rates = jnp.where(line == p, rates_ref[p], rates)

    pl.semaphore_wait(barrier, 6)

    started = []

    def copy(index, src, dst, device):
        return pltpu.make_async_remote_copy(
            src_ref=src,
            dst_ref=dst,
            send_sem=send_sem.at[index],
            recv_sem=recv_sem.at[index],
            device_id=device,
            device_id_type=pl.DeviceIdType.MESH,
        )

    def send(index, src, dst, device):
        one = copy(index, src, dst, device)
        one.start()
        started.append(one)

    def arrived(index, place):
        copy(index, place, place, peer_c).wait_recv()

    own_item = items.at[s, t, h]

    def z_send(k):
        send(Z + k - 1, own_item, own_item, peer_z[k])

    def z_wait(k):
        arrived(Z + k - 1, items.at[spans[k], t, h])

    def x_send(k):
        slot = items.at[spans[k] if k else s, t, h]
        send(X + k, slot, slot, peer_x)

    def x_wait(k):
        arrived(X + k, items.at[spans[k] if k else s, 1 - t, h])

    def c_send(k, crossed):
        slot = items.at[spans[k] if k else s, 1 - t if crossed else t, h]
        send((CB if crossed else CA - 1) + k, slot, slot, peer_c)

    def c_wait(k, crossed):
        slot = items.at[spans[k] if k else s, 1 - t if crossed else t, 1 - h]
        arrived((CB if crossed else CA - 1) + k, slot)

    quarters = (2 * y + low, 2 * (1 - y) + low, 2 * y + 1 - low, 2 * (1 - y) + 1 - low)

    def piece(role, k, columns):
        if k < 2:
            start = quarters[role] * (2 * UP_ROWS) + k * UP_ROWS
            return up_w.at[pl.ds(pl.multiple_of(columns * depth + start, 16), UP_ROWS), :]
        start = quarters[role] * (2 * DOWN_ROWS) + (k - 2) * DOWN_ROWS
        return down_w.at[
            pl.ds(pl.multiple_of(start, 16), DOWN_ROWS),
            pl.ds(pl.multiple_of(columns * depth, LANES), depth),
        ]

    def w_first(k):
        if k < 2:
            start = quarters[0] * (2 * UP_ROWS) + k * UP_ROWS
            src = up_hbm.at[pl.ds(pl.multiple_of(start, 16), UP_ROWS), :]
        else:
            start = quarters[0] * (2 * DOWN_ROWS) + (k - 2) * DOWN_ROWS
            src = down_hbm.at[pl.ds(pl.multiple_of(start, 16), DOWN_ROWS), :]
        send(W + k, src, piece(0, k, t), peer_x)

    def w_wait(role, k):
        arrived(W + 4 * role + k, piece(role, k, 1 - t))

    def w_pass(role, k, to, device):
        slot = piece(role, k, 1 - t)
        send(W + 4 * to + k, slot, slot, device)

    def w_relay(k):
        w_wait(0, k)
        w_pass(0, k, 1, peer_y)
        w_pass(0, k, 2, peer_z[1])

    def exchange(slot, index, count, offset=0):
        place = pl.ds(offset, count)
        send(HX + index, sent.at[slot, place], got.at[slot, place], peer_c)

    def exchanged(slot, index, count):
        arrived(HX + index, got.at[slot, pl.ds(0, count)])

    def state_of(span, part, piece_):
        return jnp.concatenate(
            [
                items[span, part, piece_, c * quarter : (c + 1) * quarter, :]
                for c in range(blocks)
            ],
            axis=1,
        ).astype(f32)

    def prepare(span, keep, out, base):
        for part in range(2):
            embed = dot(items[span, part, 0, blocks * quarter :, :], table[...], TN)
            for i in range(2):
                value = state_of(span, part, i) + embed[i * quarter : (i + 1) * quarter]
                start = base + part * half + i * quarter
                if keep:
                    hidden[start : start + quarter, :] = value
                out[start : start + quarter, :] = layer_norm(value).astype(bf16)

    def take_queries(value, start, count):
        queries[start : start + count, :] = (value.astype(bf16) * 0.125).astype(bf16)

    def attend_block(q0, count, k0, keys):
        for head in range(width // HD):
            ks = slice(head * HD, (head + 1) * HD)
            vs = slice(width + head * HD, width + (head + 1) * HD)
            score = dot(kv[k0 : k0 + keys, ks], queries[q0 : q0 + count, ks], NT)
            weights = jnp.exp(score - jnp.max(score, axis=0, keepdims=True))
            total = jnp.sum(weights, axis=0, keepdims=True)
            value = dot(kv[k0 : k0 + keys, vs], weights.astype(bf16), TN) / total
            mixed[ks, :count] = value.astype(bf16)

    def out_part(slot, count):
        sent[slot, :count, :] = dot(mixed[:, :count], out_w[...], TN).astype(bf16)

    def total_of(slot, count):
        return sent[slot, :count, :].astype(f32) + got[slot, :count, :].astype(f32)

    def ffn(source, slot, count):
        tile = 512
        for i in range(0, up_w.shape[1], tile):
            value = dot(source, up_w[:, i : i + tile])
            act[:count, i : i + tile] = jax.nn.gelu(value, approximate=True).astype(bf16)
        sent[slot, :count, :] = dot(act[:count, :], down_w[...]).astype(bf16)

    def rate_of(span):
        hots = items[span, 0, 0, blocks * quarter : blocks * quarter + 16, :].astype(f32)
        row = jnp.sum(hots * rates, axis=0, keepdims=True)
        return jnp.concatenate([row] * blocks, axis=1)

    z_send(1)
    z_send(3)
    z_send(2)
    x_send(0)
    w_first(0)
    w_first(1)
    x_wait(0)
    c_send(0, True)
    z_wait(1)
    x_send(1)
    c_send(1, False)
    for load in loads[:3]:
        load.wait()
    c_wait(0, True)
    prepare(s, True, normed, 0)
    value = dot(normed[0:rows, :], qkv_w[...])
    take_queries(value[:, :width], 0, rows)
    kv[0:rows, :] = value[:, width:].astype(bf16)
    z_wait(3)
    x_send(3)
    c_send(3, False)
    z_wait(2)
    x_send(2)
    c_send(2, False)
    w_first(2)
    w_first(3)
    w_relay(0)
    w_relay(1)
    for k in (1, 3, 2):
        x_wait(k)
        c_send(k, True)
    for k in (1, 3, 2):
        c_wait(k, False)
        c_wait(k, True)
    for load in loads[3:]:
        load.wait()

    owner, follower = owners_ref[0], owners_ref[1]
    prepare(owner, False, ctx_normed, 0)
    kv[rows : 2 * rows, :] = dot(ctx_normed[...], qkv_w[:, width:]).astype(bf16)
    attend_block(0, rows, 0, 2 * rows)
    out_part(0, rows)
    exchange(0, 0, rows)
    w_relay(2)
    w_wait(1, 1)
    w_pass(1, 1, 3, peer_z[1])
    w_wait(2, 0)
    w_pass(2, 0, 3, peer_y)
    prepare(follower, True, normed, rows)
    value = dot(normed[rows : 2 * rows, :], qkv_w[...])
    take_queries(value[:, :width], rows, rows)
    kv[2 * rows : 3 * rows, :] = value[:, width:].astype(bf16)
    attend_block(rows, rows, rows, 2 * rows)
    out_part(1, rows)
    exchange(1, 1, rows)
    w_relay(3)
    for k in (2, 3):
        w_wait(2, k)
        w_pass(2, k, 3, peer_y)

    exchanged(0, 0, rows)
    hidden[0:rows, :] = hidden[0:rows, :] + total_of(0, rows)
    normed[0:rows, :] = layer_norm(hidden[0:rows, :]).astype(bf16)
    w_wait(2, 1)
    for k in (0, 2, 3):
        w_wait(1, k)
    for k in range(4):
        w_wait(3, k)
    ffn(normed[0:rows, :], 2, rows)
    exchange(2, 2, rows)
    exchanged(1, 1, rows)
    hidden[rows:, :] = hidden[rows:, :] + total_of(1, rows)
    normed[rows:, :] = layer_norm(hidden[rows:, :]).astype(bf16)
    ffn(normed[rows:, :], 3, rows)
    exchange(3, 3, rows)

    def update(span, base, slot):
        rate = rate_of(span)
        for part in range(2):
            embed = dot(items[span, part, 0, blocks * quarter :, :], table[...], TN)
            for i in range(2):
                start = part * half + i * quarter
                here = slice(base + start, base + start + quarter)
                previous = state_of(span, part, i)
                after = hidden[here, :] + (
                    sent[slot, start : start + quarter, :].astype(f32)
                    + got[slot, start : start + quarter, :].astype(f32)
                )
                state = (previous + rate * (after - previous)).astype(bf16).astype(f32)
                value = state + embed[i * quarter : (i + 1) * quarter]
                after_state[here, :] = state
                hidden[here, :] = value
                normed[here, :] = layer_norm(value).astype(bf16)

    mine = pl.ds(pl.multiple_of(t * half, half), half)
    exchanged(2, 2, rows)
    update(s, 0, 2)
    take_queries(dot(normed[mine, :], qkv_w[:, :width]), 0, half)
    kv[0:rows, :] = dot(normed[0:rows, :], qkv_w[:, width:]).astype(bf16)
    exchanged(3, 3, rows)
    update(follower, rows, 3)
    kv[rows : 2 * rows, :] = dot(normed[rows:, :], qkv_w[:, width:]).astype(bf16)
    attend_block(0, half, 0, 2 * rows)
    out_part(4, half)
    exchange(4, 4, half)
    exchanged(4, 4, half)
    after = hidden[mine, :] + total_of(4, half)
    normed[0:half, :] = layer_norm(after).astype(bf16)
    ffn(normed[0:half, :], 5, half)
    exchange(5, 5, half)
    exchanged(5, 5, half)
    after = after + total_of(5, half)
    previous = after_state[mine, :]
    result_ref[0] = (previous + rate_of(s) * (after - previous)).astype(bf16)
    for one in started:
        one.wait_send()


def fused(frames, levels, owners, ids, w_qkv, w_out, w_up, w_down, level_table, person_table, rates):
    half, model = frames.shape[1:]
    rows = 2 * half
    width = w_out.shape[0]
    inner = w_up.shape[1]
    depth = w_up.shape[0]
    item = (model // LANES) * (half // 2) + INFO
    anywhere = pl.BlockSpec(memory_space=pl.ANY)
    bf16, f32 = jnp.bfloat16, jnp.float32
    return pl.pallas_call(
        fused_kernel,
        out_shape=jax.ShapeDtypeStruct(frames.shape, bf16),
        in_specs=[SMEM] * 3 + [VMEM] * 4 + [anywhere] * 4,
        out_specs=VMEM,
        scratch_shapes=[
            pltpu.VMEM((4, 2, 2, item, LANES), bf16),
            pltpu.VMEM((INFO, model), bf16),
            pltpu.VMEM((model, 3 * width), bf16),
            pltpu.VMEM((width, model), bf16),
            pltpu.VMEM((2 * depth, inner), bf16),
            pltpu.VMEM((inner, 2 * depth), bf16),
            pltpu.VMEM((2 * rows, model), f32),
            pltpu.VMEM((2 * rows, model), f32),
            pltpu.VMEM((2 * rows, model), bf16),
            pltpu.VMEM((rows, model), bf16),
            pltpu.VMEM((2 * rows, width), bf16),
            pltpu.VMEM((3 * rows, 2 * width), bf16),
            pltpu.VMEM((width, rows), bf16),
            pltpu.VMEM((rows, inner), bf16),
            pltpu.VMEM((6, rows, model), bf16),
            pltpu.VMEM((6, rows, model), bf16),
            pltpu.SemaphoreType.DMA((COPIES,)),
            pltpu.SemaphoreType.DMA((COPIES,)),
            pltpu.SemaphoreType.DMA((6,)),
        ],
        compiler_params=pltpu.CompilerParams(
            collective_id=2, has_side_effects=True, vmem_limit_bytes=48 * 2**20
        ),
        cost_estimate=pl.CostEstimate(
            flops=2 * model * (7 * rows * 3 * width + 5 * rows * inner),
            bytes_accessed=2 * model * (4 * width + 2 * inner),
            transcendentals=6 * rows * rows * width // HD,
        ),
        name="fused",
    )(owners, levels, rates, ids, frames, level_table, person_table, w_qkv, w_out, w_up, w_down)


def body(
    spans,
    slabs,
    frames,
    levels,
    owners,
    person_ids,
    w_qkv,
    w_out,
    w_up,
    w_down,
    level_table,
    person_table,
    blend_rates,
):
    shape = (lax.axis_size("grp"), spans, slabs, lax.axis_size("head"))
    if shape == (2, 4, 2, 2) and frames.shape == (1, LANES, 768):
        return fused(
            frames, levels, owners, person_ids, w_qkv, w_out, w_up, w_down,
            level_table, person_table, blend_rates,
        )
    level_hot = (levels[0] == jnp.arange(level_table.shape[0], dtype=jnp.int32)).astype(
        jnp.bfloat16
    )
    level_row = jnp.dot(level_hot[None, :], level_table, preferred_element_type=jnp.float32)
    person_hot = (
        person_ids[0][:, None] == jnp.arange(person_table.shape[0], dtype=jnp.int32)[None, :]
    ).astype(jnp.bfloat16)
    embed = level_row + jnp.dot(person_hot, person_table, preferred_element_type=jnp.float32)
    blend = jnp.sum(level_hot.astype(jnp.float32) * blend_rates)
    state = frames[0]
    hidden = state.astype(jnp.float32) + embed
    normed = layer_norm(hidden).astype(jnp.bfloat16)
    ups, downs = [], []
    if slabs == 2:
        normed, up, down = lax.optimization_barrier((normed, w_up, w_down))
        size = up.shape[1] // 4
        grp = lax.axis_index("grp").astype(jnp.int32)
        for i in (0, 1):
            ups += relayed(up, 1, (2 * grp + i) * size, size)
        for i in (0, 1):
            downs += relayed(down, 0, (2 * grp + i) * size, size)
    else:
        up = lax.all_gather(w_up, "tm", axis=0, tiled=True)
        down = lax.all_gather(w_down, "tm", axis=1, tiled=True)
    for step_index in range(STEPS):
        owner = owners[step_index]
        if slabs == 2:
            blocks = [normed, swap(normed, "tm")]
        else:
            blocks = [lax.all_gather(normed, "tm", axis=0, tiled=True)]
        if slabs == 2 and step_index == 0:
            context = owner_halves(*blocks, owner, spans, (ups[0], ups[2]))
            context[1] = tied(context[1], ups[1], downs[0])
        else:
            context = owner_quarters(normed, owner, spans, slabs)
        queries, own = project(w_qkv, normed, blocks)
        if slabs == 2 and step_index == 0:
            queries = tied(queries, ups[3], downs[2])
        last = () if step_index == STEPS - 1 else (embed,)
        weights = (up, down, *ups, *downs)
        state, *rest = layer(
            blend, queries, own, w_qkv, w_out, state, hidden, last, context, weights
        )
        if rest:
            hidden, normed = rest
    return state[None]


def solution(mesh):
    placed = (
        P(("grp", "span"), "tm", None),
        P(("grp", "span")),
        P("grp"),
        P(("grp", "span"), "tm"),
        P(None, None, "head"),
        P("head", None),
        P("tm", "head"),
        P("head", "tm"),
        P(),
        P(),
        P(),
    )
    return jax.shard_map(
        functools.partial(body, mesh.shape["span"], mesh.shape["tm"]),
        mesh=mesh,
        in_specs=placed,
        out_specs=P(("grp", "span"), "tm", None),
        check_vma=False,
    )
```
